32 devices in a mesh: wealth: 4 (over z), income: 8 (over y, x, core).
Axes of the slice: x: 2, y: 2, z: 4, core: 2. Of those that a mesh axis runs over, the one named last changes fastest.
Arguments:
- value_field: float32 [8192, 4096], P('income', 'wealth'), may hold values from -4.5 to 4.5
- income: float32 [8192], P('income'), may hold values from 0.5 to 2
- jump_rates: float32 [8192, 8192], P(None, 'income'), may hold values from 0 to 0.024414062, as said below
Outputs:
- value_next: float32 [8192, 4096], P('income', 'wealth')
The draws below stay inside these ranges and needn't reach their ends.
Inputs may be any that keep to these rules, and one draw needn't show every extreme that they name: jump_rates is symmetric, with nonnegative entries.
All inputs are finite; a program needn't handle non-finite values.
Results may differ from the reference program's by a relative error of at most 0.000057.
Values sent between devices are 32-bit elements; how exact they have to be, the bound alone decides.
No kernel may reach another device: no remote copies, remote signals or barrier semaphores. Data moves between devices by JAX's collectives and lax.ppermute only.
A program may use at most 192 MiB of HBM per device.

```python
import math
import jax
import jax.numpy as jnp
from jax import lax

NZ = 8192
NA = 4096


def draw_jump_rates(key, part):
    normal_draw = jax.random.normal(key, (NZ, NZ), jnp.float32)
    symmetric = (normal_draw + normal_draw.T) * 0.70710678
    levels = jnp.exp(1.5 * jnp.clip(symmetric, -4.0, 4.0))
    rates = levels * (0.487 / NZ)
    return rates


def draw_value_field(key, part):
    level_key = jax.random.fold_in(key, 11)
    common_key = jax.random.fold_in(key, 12)
    own_key = jax.random.fold_in(key, 13)
    wealth = (jnp.arange(NA) + 1).astype(jnp.float32) / NA
    profile = 2.0 * jnp.sqrt(wealth) - 1.0
    level = jax.random.uniform(level_key, (NZ, 1), jnp.float32, -1.5, 1.5)
    common = jax.random.uniform(common_key, (1, NA), jnp.float32, -0.8, 0.8)
    own = jax.random.uniform(own_key, (NZ, NA), jnp.float32, -1.0, 1.0)
    return level + profile[None, :] + common + own


def block_scale(stream_key, extent, cuts, smallest, top_value):
    factor_of, own = 1.0, jax.random.fold_in(stream_key, 6)
    for axis_at, blocks in cuts:
        heights = jnp.exp(jax.random.uniform(jax.random.fold_in(own, axis_at), (blocks,), jnp.float32, smallest / len(cuts), top_value / len(cuts)))
        factor_of = factor_of * jnp.repeat(heights, extent[axis_at] // blocks).reshape([-1 if axis == axis_at else 1 for axis in range(len(extent))])
    return factor_of


def setup_inputs(seed: int = 0) -> dict:
    streams_of = jax.random.split(jax.random.key(seed), 4)
    return {
        "value_field": draw_value_field(jax.random.fold_in(streams_of[3], 71), 0),
        "income": jnp.clip(jnp.exp(math.log(2.0) - 1.3862944 * jax.random.uniform(streams_of[1], (NZ,), jnp.float32) ** block_scale(streams_of[1], (NZ,), ((0, 8),), -0.2, 0.2)), 0.5, 2.0),
        "jump_rates": draw_jump_rates(jax.random.fold_in(streams_of[3], 71), 0),
    }


interest = 0.03
premium = 0.3
volatility = 0.5
discount = 0.05
time_step = 0.5
slope_floor = 0.2


def hamiltonian(padded, income, wealth_grid):
    step_up = padded[:, 2:] - padded[:, 1:-1]
    step_down = padded[:, 1:-1] - padded[:, :-2]
    gradient = 0.5 * (step_up + step_down)
    curvature = step_up - step_down
    clipped = jnp.maximum(gradient, slope_floor)
    consumption = 1.0 / clipped
    concave = jnp.maximum(-curvature, 1.0)
    risky_share = jnp.clip(premium * gradient / (volatility * volatility * wealth_grid[None, :] * concave), 0.0, 1.0)
    exposure = risky_share * wealth_grid[None, :]
    drift_term = income[:, None] + interest * wealth_grid[None, :] - consumption
    return (-jnp.log(clipped) + gradient * drift_term + premium * exposure * gradient
            + 0.5 * volatility * volatility * exposure * exposure * curvature)


def reference(value_field, income, jump_rates):
    wealth_grid = (jnp.arange(NA) + 1).astype(jnp.float32) / NA
    lower_edge = value_field[:, :1] - 1.0 / income[:, None]
    padded = jnp.concatenate([lower_edge, value_field, value_field[:, -1:]], axis=1)
    local_part = hamiltonian(padded, income, wealth_grid)
    jump_terms = jnp.dot(jump_rates, value_field, precision=lax.Precision.HIGHEST, preferred_element_type=jnp.float32)
    outflow = jnp.sum(jump_rates, axis=1)
    change = local_part + jump_terms - (outflow[:, None] + discount) * value_field
    return value_field + time_step * change
```

```python
import jax
import jax.numpy as jnp
from jax import lax
from jax.experimental import pallas as pl
from jax.experimental.pallas import tpu as pltpu
from jax.sharding import PartitionSpec as P


interest = 0.03
premium = 0.3
volatility = 0.5
discount = 0.05
time_step = 0.5
slope_floor = 0.2


def hamiltonian(padded, income, wealth_grid):
    step_up = padded[:, 2:] - padded[:, 1:-1]
    step_down = padded[:, 1:-1] - padded[:, :-2]
    gradient = 0.5 * (step_up + step_down)
    curvature = step_up - step_down
    clipped = jnp.maximum(gradient, slope_floor)
    consumption = 1.0 / clipped
    concave = jnp.maximum(-curvature, 1.0)
    risky_share = jnp.clip(
        premium * gradient / (volatility * volatility * wealth_grid[None, :] * concave), 0.0, 1.0
    )
    exposure = risky_share * wealth_grid[None, :]
    drift_term = income[:, None] + interest * wealth_grid[None, :] - consumption
    return (
        -jnp.log(clipped)
        + gradient * drift_term
        + premium * exposure * gradient
        + 0.5 * volatility * volatility * exposure * exposure * curvature
    )


def base_part(value_field, income, outflow):
    slab_cols = value_field.shape[1]
    count = lax.axis_size("wealth")
    index = lax.axis_index("wealth")
    up = [(i, i + 1) for i in range(count - 1)]
    down = [(j, i) for i, j in up]
    before = lax.ppermute(value_field[:, -1], "wealth", up)
    after = lax.ppermute(value_field[:, 0], "wealth", down)
    lower_edge = jnp.where(index == 0, value_field[:, 0] - 1.0 / income, before)
    upper_edge = jnp.where(index == count - 1, value_field[:, -1], after)
    padded = jnp.concatenate([lower_edge[:, None], value_field, upper_edge[:, None]], axis=1)
    wealth_grid = (index * slab_cols + jnp.arange(slab_cols) + 1).astype(jnp.float32) / (
        slab_cols * count
    )
    local_part = hamiltonian(padded, income, wealth_grid)
    return value_field + time_step * (local_part - (outflow[:, None] + discount) * value_field)


def split(a):
    high = a.astype(jnp.bfloat16)
    return high, (a - high.astype(jnp.float32)).astype(jnp.bfloat16)


def dot_cols(a, b):
    return jnp.dot(a, b, preferred_element_type=jnp.float32)


def dot_rows(a, b):
    return lax.dot_general(a, b, (((0,), (0,)), ((), ())), preferred_element_type=jnp.float32)


def add_jumps(total, rates, me, pieces, cols, tile=256):
    rows, width = total.shape
    count = len(pieces)
    values = [p for p, _, _ in pieces]
    depth = sum(p.shape[0] for p in values)

    def body(at, *refs):
        value, rate = refs[:count], refs[count : 2 * count]
        old, new, high, low = refs[2 * count :]

        @pl.when(pl.program_id(0) == 0)
        def _():
            first = 0
            for ref in value:
                last = first + ref.shape[0]
                high[first:last], low[first:last] = split(ref[...])
                first = last

        rate_high, rate_low = split(jnp.concatenate([ref[...] for ref in rate], axis=0))
        acc = dot_rows(rate_low, high[...]) + dot_rows(rate_high, low[...])
        new[...] = old[...] + time_step * (dot_rows(rate_high, high[...]) + acc)

    def rate_block(p, bits, first):
        size = p.shape[0]
        return pl.BlockSpec(
            (size, tile), lambda m, at: ((at[0] ^ bits) * (rows // size) + first // size, m)
        )

    specs = [pl.BlockSpec((p.shape[0], cols), lambda m, at: (0, 0)) for p in values]
    specs += [rate_block(*piece) for piece in pieces]
    specs += [pl.BlockSpec((tile, cols), lambda m, at: (m, 0))]
    return pl.pallas_call(
        body,
        out_shape=jax.ShapeDtypeStruct((rows, width), jnp.float32),
        grid_spec=pltpu.PrefetchScalarGridSpec(
            num_scalar_prefetch=1,
            grid=(rows // tile,),
            in_specs=specs,
            out_specs=pl.BlockSpec((tile, cols), lambda m, at: (m, 0)),
            scratch_shapes=[pltpu.VMEM((depth, cols), jnp.bfloat16)] * 2,
        ),
        input_output_aliases={1 + 2 * count: 0},
        cost_estimate=pl.CostEstimate(
            flops=6 * rows * cols * depth,
            bytes_accessed=8 * rows * cols + 4 * depth * (rows + cols),
            transcendentals=0,
        ),
        name="add_jumps",
    )(me.reshape(1), *values, *([rates] * count), total)


def partial_jumps(value_field, rates, me, bit, wide, tile=512):
    rows, cols = value_field.shape
    steps = rows // tile

    def body(at, value, rate, part, sums, high, low):
        first = (pl.program_id(0) == 0) & (pl.program_id(1) == 0)

        @pl.when(first)
        def _():
            high[...], low[...] = split(value[...])
            sums[...] = jnp.zeros_like(sums)

        block = rate[...]
        sums[...] += jnp.sum(block.reshape(tile // 8, 8, rows), axis=0)
        rate_high, rate_low = split(block)
        acc = dot_cols(rate_low, high[...]) + dot_cols(rate_high, low[...])
        part[...] = (dot_cols(rate_high, high[...]) + acc)[None]

    return pl.pallas_call(
        body,
        out_shape=(
            jax.ShapeDtypeStruct((4, rows, wide), jnp.float32),
            jax.ShapeDtypeStruct((8, rows), jnp.float32),
        ),
        grid_spec=pltpu.PrefetchScalarGridSpec(
            num_scalar_prefetch=1,
            grid=(4, steps),
            in_specs=[
                pl.BlockSpec((rows, wide), lambda q, m, at: (0, cols // wide - 1)),
                pl.BlockSpec((tile, rows), lambda q, m, at: ((at[0] ^ bit ^ (2 * q)) * steps + m, 0)),
            ],
            out_specs=(
                pl.BlockSpec((1, tile, wide), lambda q, m, at: (q, m, 0)),
                pl.BlockSpec((8, rows), lambda q, m, at: (0, 0)),
            ),
            scratch_shapes=[pltpu.VMEM((rows, wide), jnp.bfloat16)] * 2,
        ),
        cost_estimate=pl.CostEstimate(
            flops=24 * rows * rows * wide, bytes_accessed=16 * rows * (rows + 2 * wide), transcendentals=0
        ),
        name="partial_jumps",
    )(me.reshape(1), value_field, rates)


def add_last(total, plain, combined, own):
    rows, cols = total.shape
    half, wide = plain[0].shape

    def body(plain_a, plain_b, combined_a, combined_b, own_part, old, new):
        new[:half] = old[:half] + time_step * (own_part[:half] + plain_a[...] + combined_a[...])
        new[half:] = old[half:] + time_step * (own_part[half:] + plain_b[...] + combined_b[...])

    part = pl.BlockSpec((half, wide), lambda m: (0, 0))
    whole = pl.BlockSpec((rows, wide), lambda m: (0, 0))
    last = pl.BlockSpec((rows, wide), lambda m: (0, cols // wide - 1))
    return pl.pallas_call(
        body,
        grid=(1,),
        out_shape=jax.ShapeDtypeStruct((rows, cols), jnp.float32),
        in_specs=[part] * 4 + [whole, last],
        out_specs=last,
        input_output_aliases={5: 0},
        name="add_last",
    )(*plain, *combined, own, total)


def swap(x, bit):
    count = lax.axis_size("income")
    return lax.ppermute(x, "income", [(i, i ^ bit) for i in range(count)])


def local_grid(value_field, income, jump_rates):
    return step_grid(value_field, income, jump_rates)


def step_grid(value_field, income, jump_rates):
    rows, cols = value_field.shape
    half, wide = rows // 2, cols // 4
    narrow = cols - wide
    me = lax.axis_index("income")

    def add(total, items):
        return add_jumps(total, jump_rates, me, items, narrow)

    def both(v, bits, first):
        return [(v, bits, first), (swap(v, 1), bits ^ 1, first)]

    half_a, half_b = value_field[:half, :narrow], value_field[half:, :narrow]
    x_a, y_b = swap(half_a, 2), swap(half_b, 4)
    x_b, y_a = swap(half_b, 2), swap(half_a, 4)
    far_a, far_b = swap(x_a, 4), swap(y_b, 2)
    other = swap(value_field, 1)

    send, sums_send = partial_jumps(value_field, jump_rates, me, 1, wide)
    keep, sums_keep = partial_jumps(value_field, jump_rates, me, 0, wide)
    got = swap(send, 1)

    def parts(q, first):
        return keep[q, first : first + half] + got[q, first : first + half]

    first_x = swap(parts(3, 0), 2)
    first_y = swap(parts(3, half), 4)
    plain_x = swap(parts(1, 0), 2)
    plain_y = swap(parts(2, half), 4)
    comb_x = swap(parts(1, half) + first_y, 2)
    comb_y = swap(parts(2, 0) + first_x, 4)

    outflow = jnp.sum(sums_send + sums_keep, axis=0)
    total = base_part(value_field, income, outflow)
    total = add(total, [(value_field, 0, 0), (other, 1, 0)])
    total = add(total, both(x_a, 2, 0) + both(y_b, 4, half))
    total = add(total, both(x_b, 2, half) + both(y_a, 4, 0))
    total = add(total, both(far_a, 6, 0) + both(far_b, 6, half))
    return add_last(total, (plain_x, plain_y), (comb_y, comb_x), keep[0] + got[0])


def local_any(value_field, income, jump_rates):
    jump_terms = lax.psum_scatter(
        jnp.dot(
            jump_rates,
            value_field,
            precision=lax.Precision.HIGHEST,
            preferred_element_type=jnp.float32,
        ),
        "income",
        scatter_dimension=0,
        tiled=True,
    )
    outflow = jnp.sum(jump_rates, axis=0)
    return base_part(value_field, income, outflow) + time_step * jump_terms


def solution(mesh):
    grid = mesh.shape["income"] == 8
    return jax.shard_map(
        local_grid if grid else local_any,
        mesh=mesh,
        in_specs=(P("income", "wealth"), P("income"), P(None, "income")),
        out_specs=P("income", "wealth"),
        check_vma=False,
    )
```

```python
import jax
import jax.numpy as jnp
from jax import lax
from jax.experimental import pallas as pl
from jax.experimental.pallas import tpu as pltpu
from jax.sharding import PartitionSpec as P


ADD_VMEM, PART_VMEM = 28, 28

interest = 0.03
premium = 0.3
volatility = 0.5
discount = 0.05
time_step = 0.5
slope_floor = 0.2


def hamiltonian(padded, income, wealth_grid):
    step_up = padded[:, 2:] - padded[:, 1:-1]
    step_down = padded[:, 1:-1] - padded[:, :-2]
    gradient = 0.5 * (step_up + step_down)
    curvature = step_up - step_down
    clipped = jnp.maximum(gradient, slope_floor)
    consumption = 1.0 / clipped
    concave = jnp.maximum(-curvature, 1.0)
    risky_share = jnp.clip(
        premium * gradient / (volatility * volatility * wealth_grid[None, :] * concave), 0.0, 1.0
    )
    exposure = risky_share * wealth_grid[None, :]
    drift_term = income[:, None] + interest * wealth_grid[None, :] - consumption
    return (
        -jnp.log(clipped)
        + gradient * drift_term
        + premium * exposure * gradient
        + 0.5 * volatility * volatility * exposure * exposure * curvature
    )


def base_part(value_field, income, outflow):
    slab_cols = value_field.shape[1]
    count = lax.axis_size("wealth")
    index = lax.axis_index("wealth")
    up = [(i, i + 1) for i in range(count - 1)]
    down = [(j, i) for i, j in up]
    before = lax.ppermute(value_field[:, -1], "wealth", up)
    after = lax.ppermute(value_field[:, 0], "wealth", down)
    lower_edge = jnp.where(index == 0, value_field[:, 0] - 1.0 / income, before)
    upper_edge = jnp.where(index == count - 1, value_field[:, -1], after)
    padded = jnp.concatenate([lower_edge[:, None], value_field, upper_edge[:, None]], axis=1)
    wealth_grid = (index * slab_cols + jnp.arange(slab_cols) + 1).astype(jnp.float32) / (
        slab_cols * count
    )
    local_part = hamiltonian(padded, income, wealth_grid)
    return value_field + time_step * (local_part - (outflow[:, None] + discount) * value_field)


def split(a):
    high = a.astype(jnp.bfloat16)
    return high, (a - high.astype(jnp.float32)).astype(jnp.bfloat16)


def dot_cols(a, b):
    return jnp.dot(a, b, preferred_element_type=jnp.float32)


def dot_rows(a, b):
    return lax.dot_general(a, b, (((0,), (0,)), ((), ())), preferred_element_type=jnp.float32)


def add_jumps(total, rates, me, pieces, cols, parts=(), tile=256):
    rows, width = total.shape
    span = width if parts else cols
    count = len(pieces)
    values = [p for p, _, _ in pieces]
    depth = sum(p.shape[0] for p in values)

    def body(at, *refs):
        value, rate = refs[:count], refs[count : 2 * count]
        extra, (old, new, high, low) = refs[2 * count : -4], refs[-4:]

        @pl.when(pl.program_id(0) == 0)
        def _():
            first = 0
            for ref in value:
                last = first + ref.shape[0]
                high[first:last], low[first:last] = split(ref[...])
                first = last

        rate_high, rate_low = split(jnp.concatenate([ref[...] for ref in rate], axis=0))
        acc = dot_rows(rate_low, high[...]) + dot_rows(rate_high, low[...])
        new[:, :cols] = old[:, :cols] + time_step * (dot_rows(rate_high, high[...]) + acc)
        if parts:
            new[:, cols:] = old[:, cols:] + time_step * sum(ref[0] for ref in extra)

    def rate_block(p, bits, first):
        size = p.shape[0]
        return pl.BlockSpec(
            (size, tile), lambda m, at: ((at[0] ^ bits) * (rows // size) + first // size, m)
        )

    specs = [
        pl.BlockSpec((p.shape[0], cols), lambda m, at: (0, 0), pipeline_mode=pl.Buffered(1))
        for p in values
    ]
    specs += [rate_block(*piece) for piece in pieces]
    specs += [pl.BlockSpec((1, tile, width - cols), lambda m, at: (0, m, 0)) for _ in parts]
    specs += [pl.BlockSpec((tile, span), lambda m, at: (m, 0))]
    return pl.pallas_call(
        body,
        out_shape=jax.ShapeDtypeStruct((rows, width), jnp.float32),
        grid_spec=pltpu.PrefetchScalarGridSpec(
            num_scalar_prefetch=1,
            grid=(rows // tile,),
            in_specs=specs,
            out_specs=pl.BlockSpec((tile, span), lambda m, at: (m, 0)),
            scratch_shapes=[pltpu.VMEM((depth, cols), jnp.bfloat16)] * 2,
        ),
        input_output_aliases={len(specs): 0},
        cost_estimate=pl.CostEstimate(
            flops=6 * rows * cols * depth,
            bytes_accessed=8 * rows * cols + 4 * depth * (rows + cols),
            transcendentals=0,
        ),
        compiler_params=pltpu.CompilerParams(vmem_limit_bytes=ADD_VMEM << 20),
        name="add_jumps",
    )(me.reshape(1), *values, *([rates] * count), *parts, total)


def partial_jumps(value_field, rates, me, bit, wide, tile=1024):
    rows, cols = value_field.shape
    steps = rows // tile

    def body(at, value, rate, part, sums, high, low):
        first = (pl.program_id(0) == 0) & (pl.program_id(1) == 0)

        @pl.when(first)
        def _():
            high[...], low[...] = split(value[...])
            sums[...] = jnp.zeros_like(sums)

        block = rate[...]
        sums[...] += jnp.sum(block.reshape(tile // 8, 8, rows), axis=0)
        rate_high, rate_low = split(block)
        acc = dot_cols(rate_low, high[...]) + dot_cols(rate_high, low[...])
        part[...] = (dot_cols(rate_high, high[...]) + acc)[None]

    return pl.pallas_call(
        body,
        out_shape=(
            jax.ShapeDtypeStruct((4, rows, wide), jnp.float32),
            jax.ShapeDtypeStruct((8, rows), jnp.float32),
        ),
        grid_spec=pltpu.PrefetchScalarGridSpec(
            num_scalar_prefetch=1,
            grid=(4, steps),
            in_specs=[
                pl.BlockSpec((rows, wide), lambda q, m, at: (0, cols // wide - 1)),
                pl.BlockSpec((tile, rows), lambda q, m, at: ((at[0] ^ bit ^ (2 * q)) * steps + m, 0)),
            ],
            out_specs=(
                pl.BlockSpec((1, tile, wide), lambda q, m, at: (q, m, 0)),
                pl.BlockSpec((8, rows), lambda q, m, at: (0, 0)),
            ),
            scratch_shapes=[pltpu.VMEM((rows, wide), jnp.bfloat16)] * 2,
        ),
        cost_estimate=pl.CostEstimate(
            flops=24 * rows * rows * wide, bytes_accessed=16 * rows * (rows + 2 * wide), transcendentals=0
        ),
        compiler_params=pltpu.CompilerParams(vmem_limit_bytes=PART_VMEM << 20),
        name="partial_jumps",
    )(me.reshape(1), value_field, rates)


def add_last(total, before, combined):
    rows, cols = total.shape
    half, wide = combined[0].shape

    def body(first, combined_a, combined_b, old, new):
        new[:half] = first[:half] + time_step * combined_a[...]
        new[half:] = first[half:] + time_step * combined_b[...]

    part = pl.BlockSpec((half, wide), lambda m: (0, 0))
    whole = pl.BlockSpec((rows, wide), lambda m: (0, 0))
    return pl.pallas_call(
        body,
        grid=(1,),
        out_shape=jax.ShapeDtypeStruct((rows, cols), jnp.float32),
        in_specs=[whole, part, part, pl.BlockSpec(memory_space=pl.ANY)],
        out_specs=pl.BlockSpec((rows, wide), lambda m: (0, cols // wide - 1)),
        input_output_aliases={3: 0},
        compiler_params=pltpu.CompilerParams(vmem_limit_bytes=16 << 20),
        name="add_last",
    )(before, *combined, total)


def swap(x, bit):
    count = lax.axis_size("income")
    return lax.ppermute(x, "income", [(i, i ^ bit) for i in range(count)])


def local_grid(value_field, income, jump_rates):
    return step_grid(value_field, income, jump_rates)


def step_grid(value_field, income, jump_rates):
    rows, cols = value_field.shape
    half, wide = rows // 2, cols // 4
    narrow = cols - wide
    me = lax.axis_index("income")

    def add(total, items, parts=()):
        return add_jumps(total, jump_rates, me, items, narrow, parts)

    def both(v, bits, first):
        return [(v, bits, first), (swap(v, 1), bits ^ 1, first)]

    whole, half_a = lax.optimization_barrier((value_field, value_field[:half, :narrow]))
    half_b = whole[half:, :narrow]
    x_a, y_a = swap(half_a, 2), swap(half_a, 4)
    x_b, y_b = swap(half_b, 2), swap(half_b, 4)
    far_a, far_b = swap(x_a, 4), swap(y_b, 2)
    other = swap(value_field, 1)

    send, sums_send = partial_jumps(value_field, jump_rates, me, 1, wide)
    keep, sums_keep = partial_jumps(value_field, jump_rates, me, 0, wide)
    got = swap(send, 1)

    def parts(q, first):
        return keep[q, first : first + half] + got[q, first : first + half]

    first_x = swap(parts(3, 0), 2)
    first_y = swap(parts(3, half), 4)
    plain_x = swap(parts(1, 0), 2)
    plain_y = swap(parts(2, half), 4)
    comb_x = swap(parts(1, half) + first_y, 2)
    comb_y = swap(parts(2, 0) + first_x, 4)

    outflow = jnp.sum(sums_send + sums_keep, axis=0)
    total = base_part(value_field, income, outflow)
    total = add(total, [(value_field, 0, 0), (other, 1, 0)], (keep, got))
    total = add(total, both(x_a, 2, 0) + both(y_a, 4, 0))
    total = add(total, both(x_b, 2, half) + both(y_b, 4, half))
    total = add(total, both(far_a, 6, 0))
    total = add(total, both(far_b, 6, half))
    plain = jnp.concatenate([plain_x, plain_y], axis=0)
    before = total[:, narrow:] + time_step * plain
    return add_last(total, before, (comb_y, comb_x))


def local_any(value_field, income, jump_rates):
    jump_terms = lax.psum_scatter(
        jnp.dot(
            jump_rates,
            value_field,
            precision=lax.Precision.HIGHEST,
            preferred_element_type=jnp.float32,
        ),
        "income",
        scatter_dimension=0,
        tiled=True,
    )
    outflow = jnp.sum(jump_rates, axis=0)
    return base_part(value_field, income, outflow) + time_step * jump_terms


def solution(mesh):
    grid = mesh.shape["income"] == 8
    return jax.shard_map(
        local_grid if grid else local_any,
        mesh=mesh,
        in_specs=(P("income", "wealth"), P("income"), P(None, "income")),
        out_specs=P("income", "wealth"),
        check_vma=False,
    )
```

```python
import jax
import jax.numpy as jnp
from jax import lax
from jax.experimental import pallas as pl
from jax.experimental.pallas import tpu as pltpu
from jax.sharding import PartitionSpec as P


ADD_VMEM, PART_VMEM = 28, 28

interest = 0.03
premium = 0.3
volatility = 0.5
discount = 0.05
time_step = 0.5
slope_floor = 0.2


def hamiltonian(padded, income, wealth_grid):
    step_up = padded[:, 2:] - padded[:, 1:-1]
    step_down = padded[:, 1:-1] - padded[:, :-2]
    gradient = 0.5 * (step_up + step_down)
    curvature = step_up - step_down
    clipped = jnp.maximum(gradient, slope_floor)
    consumption = 1.0 / clipped
    concave = jnp.maximum(-curvature, 1.0)
    risky_share = jnp.clip(
        premium * gradient / (volatility * volatility * wealth_grid[None, :] * concave), 0.0, 1.0
    )
    exposure = risky_share * wealth_grid[None, :]
    drift_term = income[:, None] + interest * wealth_grid[None, :] - consumption
    return (
        -jnp.log(clipped)
        + gradient * drift_term
        + premium * exposure * gradient
        + 0.5 * volatility * volatility * exposure * exposure * curvature
    )


def base_part(value_field, income, outflow):
    slab_cols = value_field.shape[1]
    count = lax.axis_size("wealth")
    index = lax.axis_index("wealth")
    up = [(i, i + 1) for i in range(count - 1)]
    down = [(j, i) for i, j in up]
    before = lax.ppermute(value_field[:, -1], "wealth", up)
    after = lax.ppermute(value_field[:, 0], "wealth", down)
    lower_edge = jnp.where(index == 0, value_field[:, 0] - 1.0 / income, before)
    upper_edge = jnp.where(index == count - 1, value_field[:, -1], after)
    padded = jnp.concatenate([lower_edge[:, None], value_field, upper_edge[:, None]], axis=1)
    wealth_grid = (index * slab_cols + jnp.arange(slab_cols) + 1).astype(jnp.float32) / (
        slab_cols * count
    )
    local_part = hamiltonian(padded, income, wealth_grid)
    return value_field + time_step * (local_part - (outflow[:, None] + discount) * value_field)


def split(a):
    high = a.astype(jnp.bfloat16)
    return high, (a - high.astype(jnp.float32)).astype(jnp.bfloat16)


def dot_cols(a, b):
    return jnp.dot(a, b, preferred_element_type=jnp.float32)


def dot_rows(a, b):
    return lax.dot_general(a, b, (((0,), (0,)), ((), ())), preferred_element_type=jnp.float32)


def add_jumps(total, rates, me, pieces, cols, parts=(), tile=256):
    rows, width = total.shape
    span = width if parts else cols
    count = len(pieces)
    values = [p for p, _, _ in pieces]
    depth = sum(p.shape[0] for p in values)

    def body(at, *refs):
        value, rate = refs[:count], refs[count : 2 * count]
        extra, (old, new, high, low) = refs[2 * count : -4], refs[-4:]

        @pl.when(pl.program_id(0) == 0)
        def _():
            first = 0
            for ref in value:
                last = first + ref.shape[0]
                high[first:last], low[first:last] = split(ref[...])
                first = last

        rate_high, rate_low = split(jnp.concatenate([ref[...] for ref in rate], axis=0))
        acc = dot_rows(rate_low, high[...]) + dot_rows(rate_high, low[...])
        new[:, :cols] = old[:, :cols] + time_step * (dot_rows(rate_high, high[...]) + acc)
        if parts:
            new[:, cols:] = old[:, cols:] + time_step * sum(ref[0] for ref in extra)

    def rate_block(p, bits, first):
        size = p.shape[0]
        return pl.BlockSpec(
            (size, tile), lambda m, at: ((at[0] ^ bits) * (rows // size) + first // size, m)
        )

    specs = [
        pl.BlockSpec((p.shape[0], cols), lambda m, at: (0, 0), pipeline_mode=pl.Buffered(1))
        for p in values
    ]
    specs += [rate_block(*piece) for piece in pieces]
    specs += [pl.BlockSpec((1, tile, width - cols), lambda m, at: (0, m, 0)) for _ in parts]
    specs += [pl.BlockSpec((tile, span), lambda m, at: (m, 0))]
    return pl.pallas_call(
        body,
        out_shape=jax.ShapeDtypeStruct((rows, width), jnp.float32),
        grid_spec=pltpu.PrefetchScalarGridSpec(
            num_scalar_prefetch=1,
            grid=(rows // tile,),
            in_specs=specs,
            out_specs=pl.BlockSpec((tile, span), lambda m, at: (m, 0)),
            scratch_shapes=[pltpu.VMEM((depth, cols), jnp.bfloat16)] * 2,
        ),
        input_output_aliases={len(specs): 0},
        cost_estimate=pl.CostEstimate(
            flops=6 * rows * cols * depth,
            bytes_accessed=8 * rows * cols + 4 * depth * (rows + cols),
            transcendentals=0,
        ),
        compiler_params=pltpu.CompilerParams(vmem_limit_bytes=ADD_VMEM << 20),
        name="add_jumps",
    )(me.reshape(1), *values, *([rates] * count), *parts, total)


def partial_jumps(value_field, rates, me, bit, wide, tile=1024):
    rows, cols = value_field.shape
    steps = rows // tile

    def body(at, value, rate, part, sums, high, low):
        first = (pl.program_id(0) == 0) & (pl.program_id(1) == 0)

        @pl.when(first)
        def _():
            high[...], low[...] = split(value[...])
            sums[...] = jnp.zeros_like(sums)

        block = rate[...]
        sums[...] += jnp.sum(block.reshape(tile // 8, 8, rows), axis=0)
        rate_high, rate_low = split(block)
        acc = dot_cols(rate_low, high[...]) + dot_cols(rate_high, low[...])
        part[...] = (dot_cols(rate_high, high[...]) + acc)[None]

    return pl.pallas_call(
        body,
        out_shape=(
            jax.ShapeDtypeStruct((4, rows, wide), jnp.float32),
            jax.ShapeDtypeStruct((8, rows), jnp.float32),
        ),
        grid_spec=pltpu.PrefetchScalarGridSpec(
            num_scalar_prefetch=1,
            grid=(4, steps),
            in_specs=[
                pl.BlockSpec((rows, wide), lambda q, m, at: (0, cols // wide - 1)),
                pl.BlockSpec((tile, rows), lambda q, m, at: ((at[0] ^ bit ^ (2 * q)) * steps + m, 0)),
            ],
            out_specs=(
                pl.BlockSpec((1, tile, wide), lambda q, m, at: (q, m, 0)),
                pl.BlockSpec((8, rows), lambda q, m, at: (0, 0)),
            ),
            scratch_shapes=[pltpu.VMEM((rows, wide), jnp.bfloat16)] * 2,
        ),
        cost_estimate=pl.CostEstimate(
            flops=24 * rows * rows * wide, bytes_accessed=16 * rows * (rows + 2 * wide), transcendentals=0
        ),
        compiler_params=pltpu.CompilerParams(vmem_limit_bytes=PART_VMEM << 20),
        name="partial_jumps",
    )(me.reshape(1), value_field, rates)


def add_last(total, before, combined):
    rows, cols = total.shape
    half, wide = combined[0].shape

    def body(first, combined_a, combined_b, old, new):
        new[:half] = first[:half] + time_step * combined_a[...]
        new[half:] = first[half:] + time_step * combined_b[...]

    part = pl.BlockSpec((half, wide), lambda m: (0, 0))
    whole = pl.BlockSpec((rows, wide), lambda m: (0, 0))
    return pl.pallas_call(
        body,
        grid=(1,),
        out_shape=jax.ShapeDtypeStruct((rows, cols), jnp.float32),
        in_specs=[whole, part, part, pl.BlockSpec(memory_space=pl.ANY)],
        out_specs=pl.BlockSpec((rows, wide), lambda m: (0, cols // wide - 1)),
        input_output_aliases={3: 0},
        compiler_params=pltpu.CompilerParams(vmem_limit_bytes=16 << 20),
        name="add_last",
    )(before, *combined, total)


def half_rows(value_field, first, cols, chunks=8):
    half = value_field.shape[0] // 2
    size = half // chunks

    def body(whole, part, buffer, sems):
        loads, stores = [], []
        for k in range(chunks):
            span = pl.ds(k * size, size)
            source = whole.at[pl.ds(first + k * size, size), pl.ds(0, cols)]
            loads.append(pltpu.make_async_copy(source, buffer.at[span], sems.at[k]))
            stores.append(pltpu.make_async_copy(buffer.at[span], part.at[span], sems.at[chunks + k]))
        for load in loads:
            load.start()
        for load, store in zip(loads, stores):
            load.wait()
            store.start()
        for store in stores:
            store.wait()

    return pl.pallas_call(
        body,
        out_shape=jax.ShapeDtypeStruct((half, cols), jnp.float32),
        in_specs=[pl.BlockSpec(memory_space=pl.ANY)],
        out_specs=pl.BlockSpec(memory_space=pl.ANY),
        scratch_shapes=[pltpu.VMEM((half, cols), jnp.float32), pltpu.SemaphoreType.DMA((2 * chunks,))],
        compiler_params=pltpu.CompilerParams(vmem_limit_bytes=8 << 20),
        name="half_rows",
    )(value_field)


def swap(x, bit):
    count = lax.axis_size("income")
    return lax.ppermute(x, "income", [(i, i ^ bit) for i in range(count)])


def local_grid(value_field, income, jump_rates):
    return step_grid(value_field, income, jump_rates)


def step_grid(value_field, income, jump_rates):
    rows, cols = value_field.shape
    half, wide = rows // 2, cols // 4
    narrow = cols - wide
    me = lax.axis_index("income")

    def add(total, items, parts=()):
        return add_jumps(total, jump_rates, me, items, narrow, parts)

    def both(v, bits, first):
        return [(v, bits, first), (swap(v, 1), bits ^ 1, first)]

    half_a = half_rows(value_field, 0, narrow)
    half_b = half_rows(value_field, half, narrow)
    x_a, y_a = swap(half_a, 2), swap(half_a, 4)
    x_b, y_b = swap(half_b, 2), swap(half_b, 4)
    far_a, far_b = swap(x_a, 4), swap(y_b, 2)
    other = swap(value_field, 1)

    send, sums_send = partial_jumps(value_field, jump_rates, me, 1, wide)
    keep, sums_keep = partial_jumps(value_field, jump_rates, me, 0, wide)
    got = swap(send, 1)

    def parts(q, first):
        return keep[q, first : first + half] + got[q, first : first + half]

    first_x = swap(parts(3, 0), 2)
    first_y = swap(parts(3, half), 4)
    plain_x = swap(parts(1, 0), 2)
    plain_y = swap(parts(2, half), 4)
    comb_x = swap(parts(1, half) + first_y, 2)
    comb_y = swap(parts(2, 0) + first_x, 4)

    outflow = jnp.sum(sums_send + sums_keep, axis=0)
    total = base_part(value_field, income, outflow)
    total = add(total, [(value_field, 0, 0), (other, 1, 0)], (keep, got))
    total = add(total, both(x_a, 2, 0) + both(y_a, 4, 0))
    total = add(total, both(x_b, 2, half) + both(y_b, 4, half))
    total = add(total, both(far_a, 6, 0))
    total = add(total, both(far_b, 6, half))
    plain = jnp.concatenate([plain_x, plain_y], axis=0)
    before = total[:, narrow:] + time_step * plain
    return add_last(total, before, (comb_y, comb_x))


def local_any(value_field, income, jump_rates):
    jump_terms = lax.psum_scatter(
        jnp.dot(
            jump_rates,
            value_field,
            precision=lax.Precision.HIGHEST,
            preferred_element_type=jnp.float32,
        ),
        "income",
        scatter_dimension=0,
        tiled=True,
    )
    outflow = jnp.sum(jump_rates, axis=0)
    return base_part(value_field, income, outflow) + time_step * jump_terms


def solution(mesh):
    grid = mesh.shape["income"] == 8
    return jax.shard_map(
        local_grid if grid else local_any,
        mesh=mesh,
        in_specs=(P("income", "wealth"), P("income"), P(None, "income")),
        out_specs=P("income", "wealth"),
        check_vma=False,
    )
```
